32 devices in a mesh: grp: 2 (over y), row: 8 (over z, x), key: 2 (over core).
Axes of the slice: x: 2, y: 2, z: 4, core: 2. Of those that a mesh axis runs over, the one named last changes fastest.
Arguments:
- query: bfloat16 [32, 768, 128], P(('grp', 'row'), 'key'), parts along dimension 0, may hold values from -8 to 8
- keys: bfloat16 [32, 768, 128], P(('grp', 'row'), 'key'), parts along dimension 0, may hold values from -8 to 8
- values: bfloat16 [32, 768, 128], P(('grp', 'row'), 'key'), parts along dimension 0, may hold values from -6 to 6
- gate_logits: bfloat16 [32, 768, 128], P(('grp', 'row'), 'key'), parts along dimension 0, may hold values from -8 to 8
- pair_bias: bfloat16 [4, 1536, 768], P(None, ('grp', 'row'), 'key'), parts along dimension 1, may hold values from -6 to 6
- key_mask: int32 [1536], P(('grp', 'key')), parts along dimension 0, may hold values 0 or 1
- grad_out: bfloat16 [32, 768, 128], P(('grp', 'row'), 'key'), parts along dimension 0, may hold values from -6 to 6
Outputs:
- grad_query: bfloat16 [32, 768, 128], P(('grp', 'row'), 'key'), parts along dimension 0
- grad_keys: bfloat16 [32, 768, 128], P(('grp', 'row'), 'key'), parts along dimension 0
- grad_values: bfloat16 [32, 768, 128], P(('grp', 'row'), 'key'), parts along dimension 0
- grad_gate: bfloat16 [32, 768, 128], P(('grp', 'row'), 'key'), parts along dimension 0
- grad_bias: float32 [4, 1536, 768], P(None, ('grp', 'row'), 'key'), parts along dimension 1
The draws below stay inside these ranges and needn't reach their ends.
There are 2 independent parts, one for each index of `grp`. The reference program is written for one: setup_inputs(seed, part) draws one part's arguments, and reference() takes and returns one part's arrays. A program takes and returns all parts, laid end to end along the dimension named above; each array names one. Nothing has to cross between parts.
All inputs are finite; a program needn't handle non-finite values. No bound on the sum of `key_mask` on one device may be relied on, other than what follows from the above.
Results may differ from the reference program's by a relative error of at most 0.024.
Values may be sent and summed in bfloat16 or wider, within the bound.
A program may use at most 64 MiB of HBM per device.

```python
import math
import jax
import jax.numpy as jnp
from jax import lax

HEADS = 4
HEAD_DIM = 32
C = 128
N = 768
ROWS = 16


def pair_draw(key):
    key_query, key_keys = jax.random.split(jax.random.fold_in(key, 17), 2)
    query = jnp.clip(jax.random.normal(key_query, (ROWS, N, C), jnp.float32), -6.0, 6.0)
    keyset = jnp.clip(jax.random.normal(key_keys, (ROWS, N, C), jnp.float32), -6.0, 6.0)
    return (query, keyset)


def draw_query(key, part):
    return pair_draw(key)[0].astype(jnp.bfloat16)


def draw_keys(key, part):
    return pair_draw(key)[1].astype(jnp.bfloat16)


def with_ends(values, key, least, high):
    longest = values.shape.index(max(values.shape))
    spots = []
    for shift in (0, 1):
        where = [jax.random.randint(jax.random.fold_in(key, axis), (), 0, length) for axis, length in enumerate(values.shape)]
        where[longest] = (where[longest] + shift) % values.shape[longest]
        spots.append(tuple(where))
    return values.at[spots[0]].set(least).at[spots[1]].set(high)


def steps_of(key, dims, cuts, low, top_value):
    factor_of, own = 1.0, jax.random.fold_in(key, 6)
    for axis_at, shards_of in cuts:
        heights = jnp.exp(jax.random.uniform(jax.random.fold_in(own, axis_at), (shards_of,), jnp.float32, low / len(cuts), top_value / len(cuts)))
        factor_of = factor_of * jnp.repeat(heights, dims[axis_at] // shards_of).reshape([-1 if axis == axis_at else 1 for axis in range(len(dims))])
    return factor_of


def gaussian(own_key, dims, deviation, bound, shards=(), dtype=jnp.bfloat16):
    drawn = deviation * jax.random.normal(own_key, dims, jnp.float32)
    if shards:
        drawn = drawn * steps_of(own_key, dims, shards, -0.22, 0.18)
    return jnp.clip(drawn, -bound, bound).astype(dtype)


def setup_inputs(seed: int = 0, part: int = 0) -> dict:
    seeds = jax.random.split(jax.random.key(seed), 8)
    own_keys = jax.random.split(jax.random.fold_in(seeds[7], part), 8)
    return {
        "query": draw_query(jax.random.fold_in(jax.random.fold_in(seeds[7], part), 71), part),
        "keys": draw_keys(jax.random.fold_in(jax.random.fold_in(seeds[7], part), 71), part),
        "values": gaussian(own_keys[2], (ROWS, N, C), 1.0, 6.0, ((0, 8), (1, 2))),
        "gate_logits": gaussian(own_keys[3], (ROWS, N, C), 2.0, 8.0, ((0, 8), (1, 2))),
        "pair_bias": gaussian(own_keys[4], (HEADS, N, N), 1.0, 6.0, ((1, 8), (2, 2))),
        "key_mask": with_ends((jax.random.randint(own_keys[5], (N,), 0, 4) < 3).astype(jnp.int32), jax.random.fold_in(own_keys[5], 1), 0, 1),
        "grad_out": gaussian(own_keys[6], (ROWS, N, C), 1.0, 6.0, ((0, 8), (1, 2))),
    }


def reference(query, keys, values, gate_logits, pair_bias, key_mask, grad_out):
    scaling = 1.0 / math.sqrt(HEAD_DIM)
    bias_full = pair_bias.astype(jnp.float32) + 1000000000.0 * (key_mask.astype(jnp.float32) - 1.0)[None, None, :]

    def one_row(grad_acc, inputs):
        query_row, key_row, value_row, gate_row, cot_row = inputs
        query_heads = query_row.astype(jnp.float32).reshape(N, HEADS, HEAD_DIM)
        key_heads = key_row.astype(jnp.float32).reshape(N, HEADS, HEAD_DIM)
        value_heads = value_row.astype(jnp.float32).reshape(N, HEADS, HEAD_DIM)
        logits = jnp.einsum('jhd,khd->hjk', query_heads, key_heads) * scaling + bias_full
        row_max = lax.optimization_barrier(jnp.max(logits, axis=-1, keepdims=True))
        expo = jnp.exp(logits - row_max)
        softmax_out = expo / lax.optimization_barrier(jnp.sum(expo, axis=-1, keepdims=True))
        softmax_low = softmax_out.astype(jnp.bfloat16)
        attended = jnp.einsum('hjk,khd->jhd', softmax_low.astype(jnp.float32), value_heads).reshape(N, C)
        gate_sig = jax.nn.sigmoid(gate_row.astype(jnp.float32))
        cot_float = cot_row.astype(jnp.float32)
        d_attended = (cot_float * gate_sig).astype(jnp.bfloat16)
        gate_delta = (cot_float * attended * gate_sig * (1.0 - gate_sig)).astype(jnp.bfloat16)
        upstream = d_attended.astype(jnp.float32).reshape(N, HEADS, HEAD_DIM)
        value_delta = jnp.einsum('hjk,jhd->khd', softmax_low.astype(jnp.float32), upstream).reshape(N, C).astype(jnp.bfloat16)
        d_probs = jnp.einsum('jhd,khd->hjk', upstream, value_heads)
        inner = lax.optimization_barrier(jnp.sum(upstream * attended.reshape(N, HEADS, HEAD_DIM), axis=-1)).T
        d_logits = softmax_out * (d_probs - inner[:, :, None])
        d_low = d_logits.astype(jnp.bfloat16).astype(jnp.float32)
        query_delta = (jnp.einsum('hjk,khd->jhd', d_low, key_heads) * scaling).reshape(N, C).astype(jnp.bfloat16)
        key_delta = (jnp.einsum('hjk,jhd->khd', d_low, query_heads) * scaling).reshape(N, C).astype(jnp.bfloat16)
        return (grad_acc + d_logits, (query_delta, key_delta, value_delta, gate_delta))
    empty_grad = jnp.zeros((HEADS, N, N), jnp.float32)
    grad_bias, results = lax.scan(one_row, empty_grad, (query, keys, values, gate_logits, grad_out))
    return (results[0], results[1], results[2], results[3], grad_bias)
```

```python
import functools
import math

import jax
import jax.numpy as jnp
from jax import lax
from jax.experimental import pallas as pl
from jax.experimental.pallas import tpu as pltpu
from jax.sharding import PartitionSpec as P


def combined_all(value, axis, join):
    pieces = jax.tree.map(lambda part: lax.all_gather(part, axis), value)
    head = jax.tree.map(lambda part: part[0], pieces)
    tail = jax.tree.map(lambda part: part[1:], pieces)
    subtotal, _ = lax.scan(lambda subtotal, slab: (join(subtotal, slab), None), head, tail)
    return subtotal


def combine_stats(first, second):
    joint_max = jnp.maximum(first[0], second[0])
    joint_total = first[1] * jnp.exp(first[0] - joint_max) + second[1] * jnp.exp(
        second[0] - joint_max
    )
    return (joint_max, joint_total)


def shards(query, keys, values, gate_logits, pair_bias, key_mask, grad_out):
    row_count, key_count, channels = query.shape
    head_count = pair_bias.shape[0]
    head_size = channels // head_count
    scaling = 1.0 / math.sqrt(head_size)
    query_all, gate_all, cot_all = (
        lax.all_gather(query, "key", axis=1, tiled=True),
        lax.all_gather(gate_logits, "key", axis=1, tiled=True),
        lax.all_gather(grad_out, "key", axis=1, tiled=True),
    )
    query_count = query_all.shape[1]
    bias_all = lax.all_gather(pair_bias, "row", axis=1, tiled=True)
    mask_add = 1000000000.0 * (key_mask.astype(jnp.float32) - 1.0)
    bias_full = bias_all.astype(jnp.float32) + mask_add[None, None, :]

    def one_row(grad_acc, inputs):
        query_row, key_row, value_row, gate_row, cot_row, gate_own, cot_own = inputs
        query_heads = query_row.reshape(query_count, head_count, head_size)
        key_heads = key_row.reshape(key_count, head_count, head_size)
        value_heads = value_row.reshape(key_count, head_count, head_size)
        logits = (
            jnp.einsum("jhd,khd->hjk", query_heads, key_heads, preferred_element_type=jnp.float32)
            * scaling
            + bias_full
        )
        local_max = jnp.max(logits, axis=-1)
        local_total = jnp.sum(jnp.exp(logits - local_max[:, :, None]), axis=-1)
        row_max, row_total = combined_all((local_max, local_total), "key", combine_stats)
        softmax_out = jnp.exp(logits - row_max[:, :, None]) / row_total[:, :, None]
        softmax_low = softmax_out.astype(jnp.bfloat16)
        partial_out = jnp.einsum(
            "hjk,khd->jhd", softmax_low, value_heads, preferred_element_type=jnp.float32
        ).reshape(query_count, channels)
        gate_sig = jax.nn.sigmoid(gate_row.astype(jnp.float32))
        d_attended = (cot_row.astype(jnp.float32) * gate_sig).astype(jnp.bfloat16)
        upstream = d_attended.reshape(query_count, head_count, head_size)
        d_probs = jnp.einsum(
            "jhd,khd->hjk", upstream, value_heads, preferred_element_type=jnp.float32
        )
        own_out = lax.psum_scatter(partial_out, "key", scatter_dimension=0, tiled=True)
        inner = lax.psum(jnp.sum(softmax_low * d_probs, axis=-1), "key")
        own_sig = jax.nn.sigmoid(gate_own.astype(jnp.float32))
        gate_delta = (cot_own.astype(jnp.float32) * own_out * own_sig * (1.0 - own_sig)).astype(
            jnp.bfloat16
        )
        d_logits = softmax_out * (d_probs - inner[:, :, None])
        d_low = d_logits.astype(jnp.bfloat16)
        query_term = jnp.einsum(
            "hjk,khd->jhd", d_low, key_heads, preferred_element_type=jnp.float32
        ).reshape(query_count, channels)
        query_delta = (
            lax.psum_scatter(query_term, "key", scatter_dimension=0, tiled=True) * scaling
        ).astype(jnp.bfloat16)
        key_delta = (
            (
                jnp.einsum("hjk,jhd->khd", d_low, query_heads, preferred_element_type=jnp.float32)
                * scaling
            )
            .reshape(key_count, channels)
            .astype(jnp.bfloat16)
        )
        value_delta = (
            jnp.einsum("hjk,jhd->khd", softmax_low, upstream, preferred_element_type=jnp.float32)
            .reshape(key_count, channels)
            .astype(jnp.bfloat16)
        )
        return (grad_acc + d_logits, (query_delta, key_delta, value_delta, gate_delta))

    inputs_all = (query_all, keys, values, gate_all, cot_all, gate_logits, grad_out)
    empty_grad = jnp.zeros((head_count, query_count, key_count), jnp.float32)
    grad_acc, results = lax.scan(one_row, empty_grad, inputs_all)
    grad_bias = lax.psum_scatter(grad_acc, "row", scatter_dimension=1, tiled=True)
    return (results[0], results[1], results[2], results[3], grad_bias)


def nt(a, b):
    return lax.dot_general(a, b, (((1,), (1,)), ((), ())), preferred_element_type=jnp.float32)


def nn(a, b):
    return lax.dot_general(a, b, (((1,), (0,)), ((), ())), preferred_element_type=jnp.float32)


def tn(a, b):
    return lax.dot_general(a, b, (((0,), (0,)), ((), ())), preferred_element_type=jnp.float32)


def fused_kernel(
    groups, pair, cores,
    q_ref, k_ref, v_ref, g_ref, o_ref, bias_ref, mask_ref,
    dq_ref, dk_ref, dv_ref, dg_ref, db_ref,
    xt, tt, mb, bb, q_tok, da_tok, gg_tok, dq_tok, dg_tok, dk_acc, dv_acc,
    sb, rb, gs, gr, ot, orecv,
    in_send, in_recv, bq_send, bq_recv, m_send, m_recv,
    bl_send, br_send, b_recv, p_send, p_recv, g_send, g_recv, o_send, o_recv,
):
    row, core = lax.axis_index("row"), lax.axis_index("key")
    zi, xi = row // pair, lax.rem(row, pair)
    heads = pair * cores
    me = xi * cores + core
    own_rows, tokens, channels = q_ref.shape
    width = channels // heads
    rows = pair * own_rows
    keys = cores * tokens
    block = bias_ref.shape[1]
    scaling = 1.0 / math.sqrt(width)

    def at_quad(other):
        return {"row": zi * pair + other // cores, "key": lax.rem(other, cores)}

    def at_z(other):
        return {"row": other * pair + xi, "key": core}

    def remote(src, dst, send, recv, where):
        return pltpu.make_async_remote_copy(
            src_ref=src, dst_ref=dst, send_sem=send, recv_sem=recv,
            device_id=where, device_id_type=pl.DeviceIdType.MESH,
        )

    barrier = pltpu.get_barrier_semaphore()
    for step in range(1, heads):
        pl.semaphore_signal(
            barrier, inc=1, device_id=at_quad(lax.rem(me + step, heads)),
            device_id_type=pl.DeviceIdType.MESH,
        )
    for step in range(1, groups):
        pl.semaphore_signal(
            barrier, inc=1, device_id=at_z(lax.rem(zi + step, groups)),
            device_id_type=pl.DeviceIdType.MESH,
        )
    pl.semaphore_wait(barrier, heads - 1 + groups - 1)

    def bias_quad(step):
        to, src = lax.rem(me + step, heads), lax.rem(me + heads - step, heads)
        out = remote(
            bias_ref.at[to], bb.at[row, core], bq_send.at[step], bq_recv.at[step], at_quad(to)
        )
        inn = remote(
            bias_ref.at[to],
            bb.at[zi * pair + src // cores, lax.rem(src, cores)],
            bq_send.at[step], bq_recv.at[step], at_quad(to),
        )
        return out, inn

    for step in range(1, heads):
        bias_quad(step)[0].start()
    for other in range(1, cores):
        to = lax.rem(core + other, cores)
        remote(
            mask_ref, mb.at[core], m_send.at[other], m_recv.at[other], {"row": row, "key": to}
        ).start()
    bb[row, core] = bias_ref[me]
    mb[core] = mask_ref[...]

    def in_quad(array, step):
        to, src = lax.rem(me + step, heads), lax.rem(me + heads - step, heads)
        out = remote(
            xt.at[array, to], tt.at[array, xi, core],
            in_send.at[array, step], in_recv.at[array, step], at_quad(to),
        )
        inn = remote(
            xt.at[array, to], tt.at[array, src // cores, lax.rem(src, cores)],
            in_send.at[array, step], in_recv.at[array, step], at_quad(to),
        )
        return out, inn

    for array, ref in enumerate((q_ref, k_ref, v_ref, g_ref, o_ref)):
        for local in range(own_rows):
            turned = jnp.transpose(ref[local].astype(jnp.float32)).astype(jnp.bfloat16)
            for head in range(heads):
                xt[array, head, local] = turned[head * width : (head + 1) * width, :]
        for step in range(1, heads):
            in_quad(array, step)[0].start()
        tt[array, xi, core] = xt[array, me]

    for step in range(1, heads):
        bias_quad(step)[1].wait_recv()

    def slab(index):
        return bb.at[pl.ds(index * pair, pair)]

    def to_left(index):
        return remote(slab(index), slab(index), bl_send.at[index], b_recv.at[index], at_z(zi - 1))

    def to_right(index):
        return remote(slab(index), slab(index), br_send.at[index], b_recv.at[index], at_z(zi + 1))

    @pl.when(zi > 0)
    def _():
        to_left(zi).start()

    @pl.when(zi < groups - 1)
    def _():
        to_right(zi).start()

    for other in range(1, cores):
        src = lax.rem(core + cores - other, cores)
        to = lax.rem(core + other, cores)
        remote(
            mask_ref, mb.at[src], m_send.at[other], m_recv.at[other], {"row": row, "key": to}
        ).wait()
    for array in range(5):
        for step in range(1, heads):
            in_quad(array, step)[1].wait_recv()

    def joined(array, index):
        at, local = index // own_rows, index % own_rows
        return jnp.concatenate([tt[array, at, c, local] for c in range(cores)], axis=1)

    for index in range(rows):
        q_tok[index] = jnp.transpose(joined(0, index).astype(jnp.float32)).astype(jnp.bfloat16)
        sig = jax.nn.sigmoid(joined(3, index).astype(jnp.float32))
        upstream = joined(4, index).astype(jnp.float32) * sig
        low = upstream.astype(jnp.bfloat16).astype(jnp.float32)
        da_tok[index] = jnp.transpose(low).astype(jnp.bfloat16)
        gg_tok[index] = jnp.transpose(upstream * (1.0 - sig))
        dk_acc[index] = jnp.zeros((width, keys), jnp.float32)
        dv_acc[index] = jnp.zeros((width, keys), jnp.float32)

    def queries(rblk):
        mask = jnp.concatenate([mb[c] for c in range(cores)], axis=1).astype(jnp.float32)
        bias = jnp.concatenate([bb[rblk, c] for c in range(cores)], axis=1).astype(jnp.float32)
        bias = bias + 1000000000.0 * (mask - 1.0)
        here = pl.ds(pl.multiple_of(rblk * block, 32), block)
        total = None
        for index in range(rows):
            kt, vt = joined(1, index), joined(2, index)
            q, da = q_tok[index, here, :], da_tok[index, here, :]
            logits = nn(q, kt) * scaling + bias
            expo = jnp.exp(logits - jnp.max(logits, axis=-1, keepdims=True))
            probs = expo * (1.0 / jnp.sum(expo, axis=-1, keepdims=True))
            low = probs.astype(jnp.bfloat16)
            attended = nt(low, vt)
            inner = jnp.sum(da.astype(jnp.float32) * attended, axis=-1, keepdims=True)
            d_logits = probs * (nn(da, vt) - inner)
            d_low = d_logits.astype(jnp.bfloat16)
            dq_tok[index, here, :] = nt(d_low, kt) * scaling
            dg_tok[index, here, :] = attended * gg_tok[index, here, :]
            dk_acc[index] += tn(q, d_low)
            dv_acc[index] += tn(da, low)
            total = d_logits if total is None else total + d_logits
        for c in range(cores):
            sb[rblk, c] = total[:, c * tokens : (c + 1) * tokens].astype(jnp.bfloat16)

    def partial_out(index):
        return remote(
            sb.at[pl.ds(index * pair, pair)], rb.at[zi], p_send.at[index], p_recv.at[zi],
            at_z(index),
        )

    orders = [sorted(range(groups), key=lambda b, a=a: abs(b - a)) for a in range(groups)]

    def turn(step, carry):
        left, right = zi - step, zi + step

        @pl.when(jnp.logical_and(step > 0, left >= 0))
        def _():
            to_left(left).wait_recv()

        @pl.when(jnp.logical_and(jnp.logical_and(step > 0, left >= 0), zi < groups - 1))
        def _():
            to_right(left).start()

        @pl.when(jnp.logical_and(step > 0, right < groups))
        def _():
            to_right(right).wait_recv()

        @pl.when(jnp.logical_and(jnp.logical_and(step > 0, right < groups), zi > 0))
        def _():
            to_left(right).start()

        index = jnp.int32(0)
        for a in range(groups):
            for s in range(groups):
                hit = jnp.logical_and(zi == a, step == s)
                index = jnp.where(hit, orders[a][s], index)
        for part in range(pair):
            queries(index * pair + part)

        @pl.when(index != zi)
        def _():
            partial_out(index).start()

        return carry

    lax.fori_loop(0, groups, turn, 0)

    for index in range(rows):
        at, local = index // own_rows, index % own_rows
        whole = (
            jnp.transpose(dq_tok[index]),
            dk_acc[index] * scaling,
            dv_acc[index],
            jnp.transpose(dg_tok[index]),
        )
        for array, value in enumerate(whole):
            value = value.astype(jnp.bfloat16)
            for c in range(cores):
                ot[at, c, array, local] = value[:, c * tokens : (c + 1) * tokens]

    def out_quad(step):
        to, src = lax.rem(me + step, heads), lax.rem(me + heads - step, heads)
        away = ot.at[to // cores, lax.rem(to, cores)]
        out = remote(away, orecv.at[me], o_send.at[step], o_recv.at[step], at_quad(to))
        inn = remote(away, orecv.at[src], o_send.at[step], o_recv.at[step], at_quad(to))
        return out, inn

    for step in range(1, heads):
        out_quad(step)[0].start()
    orecv[me] = ot[xi, core]

    for step in range(1, groups):
        src = lax.rem(zi + step, groups)
        remote(
            sb.at[pl.ds(zi * pair, pair)], rb.at[src], p_send.at[src], p_recv.at[src], at_z(src)
        ).wait_recv()
    for part in range(pair):
        for c in range(cores):
            value = sb[zi * pair + part, c].astype(jnp.float32)
            for step in range(1, groups):
                value += rb[lax.rem(zi + step, groups), part, c].astype(jnp.float32)
            gs[part, c] = value.astype(jnp.bfloat16)

    def bias_out(step):
        to, src = lax.rem(me + step, heads), lax.rem(me + heads - step, heads)
        away = gs.at[to // cores, lax.rem(to, cores)]
        out = remote(away, gr.at[me], g_send.at[step], g_recv.at[step], at_quad(to))
        inn = remote(away, gr.at[src], g_send.at[step], g_recv.at[step], at_quad(to))
        return out, inn

    for step in range(1, heads):
        bias_out(step)[0].start()
    gr[me] = gs[xi, core]

    for step in range(1, heads):
        out_quad(step)[1].wait_recv()
    for array, ref in enumerate((dq_ref, dk_ref, dv_ref, dg_ref)):
        for local in range(own_rows):
            tall = jnp.concatenate([orecv[head, array, local] for head in range(heads)], axis=0)
            ref[local] = jnp.transpose(tall.astype(jnp.float32)).astype(jnp.bfloat16)
    for step in range(1, heads):
        bias_out(step)[1].wait_recv()
    db_ref[...] = gr[...].astype(jnp.float32)

    for step in range(1, heads):
        bias_quad(step)[0].wait_send()
        out_quad(step)[0].wait_send()
        bias_out(step)[0].wait_send()
        for array in range(5):
            in_quad(array, step)[0].wait_send()
    for step in range(1, groups):
        index = lax.rem(zi + step, groups)
        partial_out(index).wait_send()
    for index in range(groups):

        @pl.when(jnp.logical_and(zi > 0, index >= zi))
        def _(index=index):
            to_left(index).wait_send()

        @pl.when(jnp.logical_and(zi < groups - 1, index <= zi))
        def _(index=index):
            to_right(index).wait_send()


def fused(row_size, cores, query, keys, values, gate_logits, pair_bias, key_mask, grad_out):
    heads, block, tokens = pair_bias.shape
    own_rows, _, channels = query.shape
    pair = heads // cores
    groups = row_size // pair
    rows, width, whole = pair * own_rows, channels // heads, cores * tokens
    blocks = groups * pair
    low, full, dma = jnp.bfloat16, jnp.float32, pltpu.SemaphoreType.DMA
    grad = jax.ShapeDtypeStruct(query.shape, low)
    vmem = pl.BlockSpec(memory_space=pltpu.VMEM)
    return pl.pallas_call(
        functools.partial(fused_kernel, groups, pair, cores),
        out_shape=(grad, grad, grad, grad, jax.ShapeDtypeStruct(pair_bias.shape, full)),
        in_specs=[vmem] * 7,
        out_specs=[vmem] * 5,
        scratch_shapes=[
            pltpu.VMEM((5, heads, own_rows, width, tokens), low),
            pltpu.VMEM((5, pair, cores, own_rows, width, tokens), low),
            pltpu.VMEM((cores, 1, tokens), jnp.int32),
            pltpu.VMEM((blocks, cores, block, tokens), low),
            pltpu.VMEM((rows, whole, width), low),
            pltpu.VMEM((rows, whole, width), low),
            pltpu.VMEM((rows, whole, width), full),
            pltpu.VMEM((rows, whole, width), full),
            pltpu.VMEM((rows, whole, width), full),
            pltpu.VMEM((rows, width, whole), full),
            pltpu.VMEM((rows, width, whole), full),
            pltpu.VMEM((blocks, cores, block, tokens), low),
            pltpu.VMEM((groups, pair, cores, block, tokens), low),
            pltpu.VMEM((pair, cores, block, tokens), low),
            pltpu.VMEM((heads, block, tokens), low),
            pltpu.VMEM((pair, cores, 4, own_rows, width, tokens), low),
            pltpu.VMEM((heads, 4, own_rows, width, tokens), low),
            dma((5, heads)), dma((5, heads)), dma((heads,)), dma((heads,)),
            dma((cores,)), dma((cores,)),
            dma((groups,)), dma((groups,)), dma((groups,)), dma((groups,)), dma((groups,)),
            dma((heads,)), dma((heads,)), dma((heads,)), dma((heads,)),
        ],
        compiler_params=pltpu.CompilerParams(
            collective_id=0, has_side_effects=True, vmem_limit_bytes=58 << 20
        ),
    )(query, keys, values, gate_logits, grad_out, pair_bias, key_mask.reshape(1, tokens))


def solution(mesh):
    in_specs = (
        P(("grp", "row"), "key", None),
        P(("grp", "row"), "key", None),
        P(("grp", "row"), "key", None),
        P(("grp", "row"), "key", None),
        P(None, ("grp", "row"), "key"),
        P(("grp", "key")),
        P(("grp", "row"), "key", None),
    )
    out_specs = (
        P(("grp", "row"), "key", None),
        P(("grp", "row"), "key", None),
        P(("grp", "row"), "key", None),
        P(("grp", "row"), "key", None),
        P(None, ("grp", "row"), "key"),
    )
    row_size, cores = mesh.shape["row"], mesh.shape["key"]

    def run(*arrays):
        heads, block, tokens = arrays[4].shape
        pair = max(heads // cores, 1)
        aligned = block % 32 == 0 and tokens % 128 == 0
        if aligned and heads == pair * cores and row_size % pair == 0:
            return fused(row_size, cores, *arrays)
        return shards(*arrays)

    return jax.shard_map(run, mesh=mesh, in_specs=in_specs, out_specs=out_specs, check_vma=False)
```

```python
import functools
import math

import jax
import jax.numpy as jnp
from jax import lax
from jax.experimental import pallas as pl
from jax.experimental.pallas import tpu as pltpu
from jax.sharding import PartitionSpec as P


def combined_all(value, axis, join):
    pieces = jax.tree.map(lambda part: lax.all_gather(part, axis), value)
    head = jax.tree.map(lambda part: part[0], pieces)
    tail = jax.tree.map(lambda part: part[1:], pieces)
    subtotal, _ = lax.scan(lambda subtotal, slab: (join(subtotal, slab), None), head, tail)
    return subtotal


def combine_stats(first, second):
    joint_max = jnp.maximum(first[0], second[0])
    joint_total = first[1] * jnp.exp(first[0] - joint_max) + second[1] * jnp.exp(
        second[0] - joint_max
    )
    return (joint_max, joint_total)


def shards(query, keys, values, gate_logits, pair_bias, key_mask, grad_out):
    row_count, key_count, channels = query.shape
    head_count = pair_bias.shape[0]
    head_size = channels // head_count
    scaling = 1.0 / math.sqrt(head_size)
    query_all, gate_all, cot_all = (
        lax.all_gather(query, "key", axis=1, tiled=True),
        lax.all_gather(gate_logits, "key", axis=1, tiled=True),
        lax.all_gather(grad_out, "key", axis=1, tiled=True),
    )
    query_count = query_all.shape[1]
    bias_all = lax.all_gather(pair_bias, "row", axis=1, tiled=True)
    mask_add = 1000000000.0 * (key_mask.astype(jnp.float32) - 1.0)
    bias_full = bias_all.astype(jnp.float32) + mask_add[None, None, :]

    def one_row(grad_acc, inputs):
        query_row, key_row, value_row, gate_row, cot_row, gate_own, cot_own = inputs
        query_heads = query_row.reshape(query_count, head_count, head_size)
        key_heads = key_row.reshape(key_count, head_count, head_size)
        value_heads = value_row.reshape(key_count, head_count, head_size)
        logits = (
            jnp.einsum("jhd,khd->hjk", query_heads, key_heads, preferred_element_type=jnp.float32)
            * scaling
            + bias_full
        )
        local_max = jnp.max(logits, axis=-1)
        local_total = jnp.sum(jnp.exp(logits - local_max[:, :, None]), axis=-1)
        row_max, row_total = combined_all((local_max, local_total), "key", combine_stats)
        softmax_out = jnp.exp(logits - row_max[:, :, None]) / row_total[:, :, None]
        softmax_low = softmax_out.astype(jnp.bfloat16)
        partial_out = jnp.einsum(
            "hjk,khd->jhd", softmax_low, value_heads, preferred_element_type=jnp.float32
        ).reshape(query_count, channels)
        gate_sig = jax.nn.sigmoid(gate_row.astype(jnp.float32))
        d_attended = (cot_row.astype(jnp.float32) * gate_sig).astype(jnp.bfloat16)
        upstream = d_attended.reshape(query_count, head_count, head_size)
        d_probs = jnp.einsum(
            "jhd,khd->hjk", upstream, value_heads, preferred_element_type=jnp.float32
        )
        own_out = lax.psum_scatter(partial_out, "key", scatter_dimension=0, tiled=True)
        inner = lax.psum(jnp.sum(softmax_low * d_probs, axis=-1), "key")
        own_sig = jax.nn.sigmoid(gate_own.astype(jnp.float32))
        gate_delta = (cot_own.astype(jnp.float32) * own_out * own_sig * (1.0 - own_sig)).astype(
            jnp.bfloat16
        )
        d_logits = softmax_out * (d_probs - inner[:, :, None])
        d_low = d_logits.astype(jnp.bfloat16)
        query_term = jnp.einsum(
            "hjk,khd->jhd", d_low, key_heads, preferred_element_type=jnp.float32
        ).reshape(query_count, channels)
        query_delta = (
            lax.psum_scatter(query_term, "key", scatter_dimension=0, tiled=True) * scaling
        ).astype(jnp.bfloat16)
        key_delta = (
            (
                jnp.einsum("hjk,jhd->khd", d_low, query_heads, preferred_element_type=jnp.float32)
                * scaling
            )
            .reshape(key_count, channels)
            .astype(jnp.bfloat16)
        )
        value_delta = (
            jnp.einsum("hjk,jhd->khd", softmax_low, upstream, preferred_element_type=jnp.float32)
            .reshape(key_count, channels)
            .astype(jnp.bfloat16)
        )
        return (grad_acc + d_logits, (query_delta, key_delta, value_delta, gate_delta))

    inputs_all = (query_all, keys, values, gate_all, cot_all, gate_logits, grad_out)
    empty_grad = jnp.zeros((head_count, query_count, key_count), jnp.float32)
    grad_acc, results = lax.scan(one_row, empty_grad, inputs_all)
    grad_bias = lax.psum_scatter(grad_acc, "row", scatter_dimension=1, tiled=True)
    return (results[0], results[1], results[2], results[3], grad_bias)


def nt(a, b):
    return lax.dot_general(a, b, (((1,), (1,)), ((), ())), preferred_element_type=jnp.float32)


def nn(a, b):
    return lax.dot_general(a, b, (((1,), (0,)), ((), ())), preferred_element_type=jnp.float32)


def tn(a, b):
    return lax.dot_general(a, b, (((0,), (0,)), ((), ())), preferred_element_type=jnp.float32)


def fused_kernel(
    groups, pair, cores,
    q_ref, k_ref, v_ref, g_ref, o_ref, bias_ref, mask_ref,
    orecv, gr,
    xt, tt, ms, mb, bb, q_tok, da_tok, dq_tok, at_tok, dk_acc, dv_acc, sb, rb, gs, ot,
    in_send, in_recv, bq_send, bq_recv, m_send, m_recv,
    bl_send, br_send, b_recv, p_send, p_recv, g_send, g_recv, o_send, o_recv, local_sem,
):
    row, core = lax.axis_index("row"), lax.axis_index("key")
    zi, xi = row // pair, lax.rem(row, pair)
    heads = pair * cores
    me = xi * cores + core
    own_rows, tokens, channels = q_ref.shape
    width = channels // heads
    rows = pair * own_rows
    keys = cores * tokens
    block = bias_ref.shape[1]
    scaling = 1.0 / math.sqrt(width)

    def at_quad(other):
        return {"row": zi * pair + other // cores, "key": lax.rem(other, cores)}

    def at_z(other):
        return {"row": other * pair + xi, "key": core}

    def remote(src, dst, send, recv, where):
        return pltpu.make_async_remote_copy(
            src_ref=src, dst_ref=dst, send_sem=send, recv_sem=recv,
            device_id=where, device_id_type=pl.DeviceIdType.MESH,
        )

    barrier = pltpu.get_barrier_semaphore()
    for step in range(1, heads):
        pl.semaphore_signal(
            barrier, inc=1, device_id=at_quad(lax.rem(me + step, heads)),
            device_id_type=pl.DeviceIdType.MESH,
        )
    for step in range(1, groups):
        pl.semaphore_signal(
            barrier, inc=1, device_id=at_z(lax.rem(zi + step, groups)),
            device_id_type=pl.DeviceIdType.MESH,
        )

    def turned(array):
        for local in range(own_rows):
            if array < 3:
                value = (q_ref, k_ref, v_ref)[array][local]
            else:
                sig = jax.nn.sigmoid(g_ref[local].astype(jnp.float32))
                value = (o_ref[local].astype(jnp.float32) * sig).astype(jnp.bfloat16)
            value = jnp.transpose(value)
            for head in range(heads):
                xt[array, head, local] = value[head * width : (head + 1) * width, :]

    own_bias = pltpu.make_async_copy(bias_ref.at[me], bb.at[row, core], local_sem.at[0])
    own_bias.start()
    ms[...] = mask_ref[...].reshape(1, tokens)
    turned(0)
    pl.semaphore_wait(barrier, heads - 1 + groups - 1)

    def bias_out_of(step):
        to = lax.rem(me + step, heads)
        return remote(
            bias_ref.at[to], bb.at[row, core], bq_send.at[step], bq_recv.at[me], at_quad(to)
        )

    def bias_from(src):
        return remote(
            bias_ref.at[src], bb.at[zi * pair + src // cores, lax.rem(src, cores)],
            bq_send.at[0], bq_recv.at[src], at_quad(src),
        )

    def mask_copy(other, src):
        return remote(
            ms, mb.at[src], m_send.at[other], m_recv.at[other],
            {"row": row, "key": lax.rem(core + other, cores)},
        )

    def token_out(array, step):
        to = lax.rem(me + step, heads)
        return remote(
            xt.at[array, to], tt.at[array, xi, core],
            in_send.at[array, step], in_recv.at[array, step], at_quad(to),
        )

    def token_in(array, step):
        src = lax.rem(me + heads - step, heads)
        return remote(
            xt.at[array, src], tt.at[array, src // cores, lax.rem(src, cores)],
            in_send.at[array, step], in_recv.at[array, step], at_quad(src),
        )

    def to_left(at):
        return remote(bb.at[at], bb.at[at], bl_send.at[at], b_recv.at[at], at_z(zi - 1))

    def to_right(at):
        return remote(bb.at[at], bb.at[at], br_send.at[at], b_recv.at[at], at_z(zi + 1))

    def launch(at):
        @pl.when(zi > 0)
        def _():
            to_left(at).start()

        @pl.when(zi < groups - 1)
        def _():
            to_right(at).start()

    def relay(distance):
        left, right = zi - distance, zi + distance
        for step in range(pair):
            part = lax.rem(xi + step, pair)

            @pl.when(left >= 0)
            def _(part=part):
                to_left(left * pair + part).wait_recv()

            @pl.when(jnp.logical_and(left >= 0, zi < groups - 1))
            def _(part=part):
                to_right(left * pair + part).start()

            @pl.when(right < groups)
            def _(part=part):
                to_right(right * pair + part).wait_recv()

            @pl.when(jnp.logical_and(right < groups, zi > 0))
            def _(part=part):
                to_left(right * pair + part).start()

    for step in range(1, heads):
        bias_out_of(step).start()
    for other in range(1, cores):
        mask_copy(other, core).start()
    mb[core] = ms[...]
    for step in range(1, heads):
        token_out(0, step).start()
    turned(1)
    for step in range(1, heads):
        token_out(1, step).start()
    own_bias.wait()
    for other in range(1, cores):
        bias_from(xi * cores + lax.rem(core + other, cores)).wait_recv()
    launch(row)
    for array in range(2, 4):
        turned(array)
        for step in range(1, heads):
            token_out(array, step).start()
    for step in range(1, pair):
        side = lax.rem(xi + step, pair)
        for other in range(cores):
            bias_from(side * cores + other).wait_recv()
        launch(zi * pair + side)
    for array in range(4):
        tt[array, xi, core] = xt[array, me]
    for other in range(1, cores):
        mask_copy(other, lax.rem(core + cores - other, cores)).wait()
    early = min(2, groups - 1)
    if early > 0:
        relay(1)
    for array in range(4):
        for step in range(1, heads):
            token_in(array, step).wait_recv()

    def joined(array, index):
        at, local = index // own_rows, index % own_rows
        return jnp.concatenate([tt[array, at, c, local] for c in range(cores)], axis=1)

    for index in range(rows):
        q_tok[index] = jnp.transpose(joined(0, index))
        da_tok[index] = jnp.transpose(joined(3, index))
        dk_acc[index] = jnp.zeros((width, keys), jnp.float32)
        dv_acc[index] = jnp.zeros((width, keys), jnp.float32)

    def queries(rblk):
        mask = jnp.concatenate([mb[c] for c in range(cores)], axis=1).astype(jnp.float32)
        bias = jnp.concatenate([bb[rblk, c] for c in range(cores)], axis=1).astype(jnp.float32)
        bias = bias + 1000000000.0 * (mask - 1.0)
        here = pl.ds(pl.multiple_of(rblk * block, 32), block)
        total = None
        for index in range(rows):
            kt, vt = joined(1, index), joined(2, index)
            q, da = q_tok[index, here, :], da_tok[index, here, :]
            logits = nn(q, kt) * scaling + bias
            expo = jnp.exp(logits - jnp.max(logits, axis=-1, keepdims=True))
            probs = expo * (1.0 / jnp.sum(expo, axis=-1, keepdims=True))
            low = probs.astype(jnp.bfloat16)
            attended = nt(low, vt)
            inner = jnp.sum(da.astype(jnp.float32) * attended, axis=-1, keepdims=True)
            d_logits = probs * (nn(da, vt) - inner)
            d_low = d_logits.astype(jnp.bfloat16)
            dq_tok[index, here, :] = nt(d_low, kt) * scaling
            at_tok[index, here, :] = attended
            dk_acc[index] += tn(q, d_low)
            dv_acc[index] += tn(da, low)
            total = d_logits if total is None else total + d_logits
        for c in range(cores):
            sb[rblk, c] = total[:, c * tokens : (c + 1) * tokens].astype(jnp.bfloat16)

    def partial_out(index, part):
        return remote(
            sb.at[index * pair + part], rb.at[zi, part], p_send.at[index, part],
            p_recv.at[zi, part], at_z(index),
        )

    orders = [
        sorted(range(groups), key=lambda b, a=a: abs(b - a) if b != a else groups)
        for a in range(groups)
    ]
    for distance in range(2, early + 1):
        relay(distance)

    def turn(step, carry):
        @pl.when(jnp.logical_and(step >= early, step < groups - 1))
        def _():
            relay(step + 1)

        index = jnp.int32(0)
        for a in range(groups):
            for s in range(groups):
                hit = jnp.logical_and(zi == a, step == s)
                index = jnp.where(hit, orders[a][s], index)
        for part in range(pair):
            queries(index * pair + part)

            @pl.when(index != zi)
            def _(part=part):
                partial_out(index, part).start()

        return carry

    lax.fori_loop(0, groups, turn, 0)

    for index in range(rows):
        at, local = index // own_rows, index % own_rows
        whole = (
            jnp.transpose(dq_tok[index]),
            dk_acc[index] * scaling,
            dv_acc[index],
            jnp.transpose(at_tok[index]),
        )
        for array, value in enumerate(whole):
            value = value.astype(jnp.bfloat16)
            for c in range(cores):
                ot[at, c, array, local] = value[:, c * tokens : (c + 1) * tokens]

    def grads_out(step):
        to = lax.rem(me + step, heads)
        return remote(
            ot.at[to // cores, lax.rem(to, cores)], orecv.at[me],
            o_send.at[step], o_recv.at[step], at_quad(to),
        )

    def grads_in(step):
        src = lax.rem(me + heads - step, heads)
        return remote(
            ot.at[src // cores, lax.rem(src, cores)], orecv.at[src],
            o_send.at[step], o_recv.at[step], at_quad(src),
        )

    def sum_out(step):
        to = lax.rem(me + step, heads)
        return remote(
            gs.at[to // cores, lax.rem(to, cores)], gr.at[me],
            g_send.at[step], g_recv.at[step], at_quad(to),
        )

    def sum_in(step):
        src = lax.rem(me + heads - step, heads)
        return remote(
            gs.at[src // cores, lax.rem(src, cores)], gr.at[src],
            g_send.at[step], g_recv.at[step], at_quad(src),
        )

    for step in range(1, heads):
        grads_out(step).start()
    own_grads = pltpu.make_async_copy(ot.at[xi, core], orecv.at[me], local_sem.at[1])
    own_grads.start()

    for part in range(pair):
        for step in range(1, groups):
            src = lax.rem(zi + step, groups)
            remote(
                sb.at[zi * pair + part], rb.at[src, part], p_send.at[src, part],
                p_recv.at[src, part], at_z(src),
            ).wait_recv()
        for c in range(cores):
            value = sb[zi * pair + part, c].astype(jnp.float32)
            for step in range(1, groups):
                value += rb[lax.rem(zi + step, groups), part, c].astype(jnp.float32)
            gs[part, c] = value.astype(jnp.bfloat16)
    for step in range(1, heads):
        sum_out(step).start()
    own_sum = pltpu.make_async_copy(gs.at[xi, core], gr.at[me], local_sem.at[2])
    own_sum.start()

    for step in range(1, heads):
        grads_in(step).wait_recv()
        sum_in(step).wait_recv()
    own_grads.wait()
    own_sum.wait()
    for step in range(1, heads):
        bias_out_of(step).wait_send()
        grads_out(step).wait_send()
        sum_out(step).wait_send()
        for array in range(4):
            token_out(array, step).wait_send()
    for step in range(1, groups):
        for part in range(pair):
            partial_out(lax.rem(zi + step, groups), part).wait_send()
    for index in range(groups):
        for part in range(pair):

            @pl.when(jnp.logical_and(zi > 0, index >= zi))
            def _(at=index * pair + part):
                to_left(at).wait_send()

            @pl.when(jnp.logical_and(zi < groups - 1, index <= zi))
            def _(at=index * pair + part):
                to_right(at).wait_send()


def write_kernel(grads, sums, g_ref, o_ref, dq_ref, dk_ref, dv_ref, dg_ref, db_ref):
    heads = grads.shape[0]
    for local in range(g_ref.shape[0]):
        for array, ref in enumerate((dq_ref, dk_ref, dv_ref, dg_ref)):
            tall = jnp.concatenate([grads[head, array, local] for head in range(heads)], axis=0)
            value = jnp.transpose(tall)
            if array == 3:
                sig = jax.nn.sigmoid(g_ref[local].astype(jnp.float32))
                scale = o_ref[local].astype(jnp.float32) * sig * (1.0 - sig)
                value = (value.astype(jnp.float32) * scale).astype(jnp.bfloat16)
            ref[local] = value
    db_ref[...] = sums[...].astype(jnp.float32)


def fused(row_size, cores, query, keys, values, gate_logits, pair_bias, key_mask, grad_out):
    heads, block, tokens = pair_bias.shape
    own_rows, _, channels = query.shape
    pair = heads // cores
    groups = row_size // pair
    rows, width, whole = pair * own_rows, channels // heads, cores * tokens
    blocks = groups * pair
    low, full, dma = jnp.bfloat16, jnp.float32, pltpu.SemaphoreType.DMA
    grad = jax.ShapeDtypeStruct(query.shape, low)
    vmem, place = pl.BlockSpec(memory_space=pltpu.VMEM), pl.BlockSpec(memory_space=pl.ANY)
    grads, sums = pl.pallas_call(
        functools.partial(fused_kernel, groups, pair, cores),
        out_shape=(
            jax.ShapeDtypeStruct((heads, 4, own_rows, width, tokens), low),
            jax.ShapeDtypeStruct((heads, block, tokens), low),
        ),
        in_specs=[vmem] * 5 + [place, vmem],
        out_specs=[place] * 2,
        scratch_shapes=[
            pltpu.VMEM((4, heads, own_rows, width, tokens), low),
            pltpu.VMEM((4, pair, cores, own_rows, width, tokens), low),
            pltpu.VMEM((1, tokens), jnp.int32),
            pltpu.VMEM((cores, 1, tokens), jnp.int32),
            pltpu.VMEM((blocks, cores, block, tokens), low),
            pltpu.VMEM((rows, whole, width), low),
            pltpu.VMEM((rows, whole, width), low),
            pltpu.VMEM((rows, whole, width), full),
            pltpu.VMEM((rows, whole, width), full),
            pltpu.VMEM((rows, width, whole), full),
            pltpu.VMEM((rows, width, whole), full),
            pltpu.VMEM((blocks, cores, block, tokens), low),
            pltpu.VMEM((groups, pair, cores, block, tokens), low),
            pltpu.VMEM((pair, cores, block, tokens), low),
            pltpu.VMEM((pair, cores, 4, own_rows, width, tokens), low),
            dma((4, heads)), dma((4, heads)), dma((heads,)), dma((heads,)),
            dma((cores,)), dma((cores,)),
            dma((blocks,)), dma((blocks,)), dma((blocks,)),
            dma((groups, pair)), dma((groups, pair)),
            dma((heads,)), dma((heads,)), dma((heads,)), dma((heads,)), dma((3,)),
        ],
        compiler_params=pltpu.CompilerParams(
            collective_id=0, has_side_effects=True, vmem_limit_bytes=58 << 20
        ),
    )(query, keys, values, gate_logits, grad_out, pair_bias, key_mask)
    return pl.pallas_call(
        write_kernel,
        out_shape=(grad, grad, grad, grad, jax.ShapeDtypeStruct(pair_bias.shape, full)),
        in_specs=[vmem] * 4,
        out_specs=[vmem] * 5,
    )(grads, sums, gate_logits, grad_out)


def solution(mesh):
    in_specs = (
        P(("grp", "row"), "key", None),
        P(("grp", "row"), "key", None),
        P(("grp", "row"), "key", None),
        P(("grp", "row"), "key", None),
        P(None, ("grp", "row"), "key"),
        P(("grp", "key")),
        P(("grp", "row"), "key", None),
    )
    out_specs = (
        P(("grp", "row"), "key", None),
        P(("grp", "row"), "key", None),
        P(("grp", "row"), "key", None),
        P(("grp", "row"), "key", None),
        P(None, ("grp", "row"), "key"),
    )
    row_size, cores = mesh.shape["row"], mesh.shape["key"]

    def run(*arrays):
        heads, block, tokens = arrays[4].shape
        pair = max(heads // cores, 1)
        aligned = block % 32 == 0 and tokens % 128 == 0
        if aligned and heads == pair * cores and row_size % pair == 0:
            return fused(row_size, cores, *arrays)
        return shards(*arrays)

    return jax.shard_map(run, mesh=mesh, in_specs=in_specs, out_specs=out_specs, check_vma=False)
```

```python
import functools
import math

import jax
import jax.numpy as jnp
from jax import lax
from jax.experimental import pallas as pl
from jax.experimental.pallas import tpu as pltpu
from jax.sharding import PartitionSpec as P


def combined_all(value, axis, join):
    pieces = jax.tree.map(lambda part: lax.all_gather(part, axis), value)
    head = jax.tree.map(lambda part: part[0], pieces)
    tail = jax.tree.map(lambda part: part[1:], pieces)
    subtotal, _ = lax.scan(lambda subtotal, slab: (join(subtotal, slab), None), head, tail)
    return subtotal


def combine_stats(first, second):
    joint_max = jnp.maximum(first[0], second[0])
    joint_total = first[1] * jnp.exp(first[0] - joint_max) + second[1] * jnp.exp(
        second[0] - joint_max
    )
    return (joint_max, joint_total)


def shards(query, keys, values, gate_logits, pair_bias, key_mask, grad_out):
    row_count, key_count, channels = query.shape
    head_count = pair_bias.shape[0]
    head_size = channels // head_count
    scaling = 1.0 / math.sqrt(head_size)
    query_all, gate_all, cot_all = (
        lax.all_gather(query, "key", axis=1, tiled=True),
        lax.all_gather(gate_logits, "key", axis=1, tiled=True),
        lax.all_gather(grad_out, "key", axis=1, tiled=True),
    )
    query_count = query_all.shape[1]
    bias_all = lax.all_gather(pair_bias, "row", axis=1, tiled=True)
    mask_add = 1000000000.0 * (key_mask.astype(jnp.float32) - 1.0)
    bias_full = bias_all.astype(jnp.float32) + mask_add[None, None, :]

    def one_row(grad_acc, inputs):
        query_row, key_row, value_row, gate_row, cot_row, gate_own, cot_own = inputs
        query_heads = query_row.reshape(query_count, head_count, head_size)
        key_heads = key_row.reshape(key_count, head_count, head_size)
        value_heads = value_row.reshape(key_count, head_count, head_size)
        logits = (
            jnp.einsum("jhd,khd->hjk", query_heads, key_heads, preferred_element_type=jnp.float32)
            * scaling
            + bias_full
        )
        local_max = jnp.max(logits, axis=-1)
        local_total = jnp.sum(jnp.exp(logits - local_max[:, :, None]), axis=-1)
        row_max, row_total = combined_all((local_max, local_total), "key", combine_stats)
        softmax_out = jnp.exp(logits - row_max[:, :, None]) / row_total[:, :, None]
        softmax_low = softmax_out.astype(jnp.bfloat16)
        partial_out = jnp.einsum(
            "hjk,khd->jhd", softmax_low, value_heads, preferred_element_type=jnp.float32
        ).reshape(query_count, channels)
        gate_sig = jax.nn.sigmoid(gate_row.astype(jnp.float32))
        d_attended = (cot_row.astype(jnp.float32) * gate_sig).astype(jnp.bfloat16)
        upstream = d_attended.reshape(query_count, head_count, head_size)
        d_probs = jnp.einsum(
            "jhd,khd->hjk", upstream, value_heads, preferred_element_type=jnp.float32
        )
        own_out = lax.psum_scatter(partial_out, "key", scatter_dimension=0, tiled=True)
        inner = lax.psum(jnp.sum(softmax_low * d_probs, axis=-1), "key")
        own_sig = jax.nn.sigmoid(gate_own.astype(jnp.float32))
        gate_delta = (cot_own.astype(jnp.float32) * own_out * own_sig * (1.0 - own_sig)).astype(
            jnp.bfloat16
        )
        d_logits = softmax_out * (d_probs - inner[:, :, None])
        d_low = d_logits.astype(jnp.bfloat16)
        query_term = jnp.einsum(
            "hjk,khd->jhd", d_low, key_heads, preferred_element_type=jnp.float32
        ).reshape(query_count, channels)
        query_delta = (
            lax.psum_scatter(query_term, "key", scatter_dimension=0, tiled=True) * scaling
        ).astype(jnp.bfloat16)
        key_delta = (
            (
                jnp.einsum("hjk,jhd->khd", d_low, query_heads, preferred_element_type=jnp.float32)
                * scaling
            )
            .reshape(key_count, channels)
            .astype(jnp.bfloat16)
        )
        value_delta = (
            jnp.einsum("hjk,jhd->khd", softmax_low, upstream, preferred_element_type=jnp.float32)
            .reshape(key_count, channels)
            .astype(jnp.bfloat16)
        )
        return (grad_acc + d_logits, (query_delta, key_delta, value_delta, gate_delta))

    inputs_all = (query_all, keys, values, gate_all, cot_all, gate_logits, grad_out)
    empty_grad = jnp.zeros((head_count, query_count, key_count), jnp.float32)
    grad_acc, results = lax.scan(one_row, empty_grad, inputs_all)
    grad_bias = lax.psum_scatter(grad_acc, "row", scatter_dimension=1, tiled=True)
    return (results[0], results[1], results[2], results[3], grad_bias)


def nt(a, b):
    return lax.dot_general(a, b, (((1,), (1,)), ((), ())), preferred_element_type=jnp.float32)


def nn(a, b):
    return lax.dot_general(a, b, (((1,), (0,)), ((), ())), preferred_element_type=jnp.float32)


def tn(a, b):
    return lax.dot_general(a, b, (((0,), (0,)), ((), ())), preferred_element_type=jnp.float32)


def fused_kernel(
    groups, pair, cores,
    q_ref, k_ref, v_ref, g_ref, o_ref, bias_ref, mask_ref,
    orecv, gr,
    xt, tt, ms, mb, bb, q_tok, da_tok, dq_tok, at_tok, dk_acc, dv_acc, sb, rb, gs, ot,
    in_send, in_recv, bq_send, bq_recv, m_send, m_recv,
    bl_send, br_send, b_recv, p_send, p_recv, g_send, g_recv, o_send, o_recv, local_sem,
):
    row, core = lax.axis_index("row"), lax.axis_index("key")
    zi, xi = row // pair, lax.rem(row, pair)
    heads = pair * cores
    me = xi * cores + core
    own_rows, tokens, channels = q_ref.shape
    width = channels // heads
    rows = pair * own_rows
    keys = cores * tokens
    block = bias_ref.shape[1]
    scaling = 1.0 / math.sqrt(width)

    def at_quad(other):
        return {"row": zi * pair + other // cores, "key": lax.rem(other, cores)}

    def at_z(other):
        return {"row": other * pair + xi, "key": core}

    def remote(src, dst, send, recv, where):
        return pltpu.make_async_remote_copy(
            src_ref=src, dst_ref=dst, send_sem=send, recv_sem=recv,
            device_id=where, device_id_type=pl.DeviceIdType.MESH,
        )

    barrier = pltpu.get_barrier_semaphore()
    for step in range(1, heads):
        pl.semaphore_signal(
            barrier, inc=1, device_id=at_quad(lax.rem(me + step, heads)),
            device_id_type=pl.DeviceIdType.MESH,
        )
    for step in range(1, groups):
        pl.semaphore_signal(
            barrier, inc=1, device_id=at_z(lax.rem(zi + step, groups)),
            device_id_type=pl.DeviceIdType.MESH,
        )

    def turned(array):
        for local in range(own_rows):
            if array < 3:
                value = (q_ref, k_ref, v_ref)[array][local]
            else:
                sig = jax.nn.sigmoid(g_ref[local].astype(jnp.float32))
                value = (o_ref[local].astype(jnp.float32) * sig).astype(jnp.bfloat16)
            value = jnp.transpose(value)
            for head in range(heads):
                xt[array, head, local] = value[head * width : (head + 1) * width, :]

    own_bias = pltpu.make_async_copy(bias_ref.at[me], bb.at[row, core], local_sem.at[0])
    own_bias.start()
    ms[...] = mask_ref[...].reshape(1, tokens)
    turned(0)
    pl.semaphore_wait(barrier, heads - 1 + groups - 1)

    def bias_out_of(step):
        to = lax.rem(me + step, heads)
        return remote(
            bias_ref.at[to], bb.at[row, core], bq_send.at[step], bq_recv.at[me], at_quad(to)
        )

    def bias_from(src):
        return remote(
            bias_ref.at[src], bb.at[zi * pair + src // cores, lax.rem(src, cores)],
            bq_send.at[0], bq_recv.at[src], at_quad(src),
        )

    def mask_copy(other, src):
        return remote(
            ms, mb.at[src], m_send.at[other], m_recv.at[other],
            {"row": row, "key": lax.rem(core + other, cores)},
        )

    def token_out(array, step):
        to = lax.rem(me + step, heads)
        return remote(
            xt.at[array, to], tt.at[array, xi, core],
            in_send.at[array, step], in_recv.at[array, step], at_quad(to),
        )

    def token_in(array, step):
        src = lax.rem(me + heads - step, heads)
        return remote(
            xt.at[array, src], tt.at[array, src // cores, lax.rem(src, cores)],
            in_send.at[array, step], in_recv.at[array, step], at_quad(src),
        )

    def to_left(at):
        return remote(bb.at[at], bb.at[at], bl_send.at[at], b_recv.at[at], at_z(zi - 1))

    def to_right(at):
        return remote(bb.at[at], bb.at[at], br_send.at[at], b_recv.at[at], at_z(zi + 1))

    def launch(at):
        @pl.when(zi > 0)
        def _():
            to_left(at).start()

        @pl.when(zi < groups - 1)
        def _():
            to_right(at).start()

    def relay(distance):
        left, right = zi - distance, zi + distance
        for step in range(pair):
            part = lax.rem(xi + step, pair)

            @pl.when(left >= 0)
            def _(part=part):
                to_left(left * pair + part).wait_recv()

            @pl.when(jnp.logical_and(left >= 0, zi < groups - 1))
            def _(part=part):
                to_right(left * pair + part).start()

            @pl.when(right < groups)
            def _(part=part):
                to_right(right * pair + part).wait_recv()

            @pl.when(jnp.logical_and(right < groups, zi > 0))
            def _(part=part):
                to_left(right * pair + part).start()

    for step in range(1, heads):
        bias_out_of(step).start()
    for other in range(1, cores):
        mask_copy(other, core).start()
    mb[core] = ms[...]
    for step in range(1, heads):
        token_out(0, step).start()
    turned(1)
    for step in range(1, heads):
        token_out(1, step).start()
    own_bias.wait()
    for other in range(1, cores):
        bias_from(xi * cores + lax.rem(core + other, cores)).wait_recv()
    launch(row)
    for array in range(2, 4):
        turned(array)
        for step in range(1, heads):
            token_out(array, step).start()
    for step in range(1, pair):
        side = lax.rem(xi + step, pair)
        for other in range(cores):
            bias_from(side * cores + other).wait_recv()
        launch(zi * pair + side)
    for array in range(4):
        tt[array, xi, core] = xt[array, me]
    for other in range(1, cores):
        mask_copy(other, lax.rem(core + cores - other, cores)).wait()
    early = min(2, groups - 1)
    if early > 0:
        relay(1)
    for array in range(4):
        for step in range(1, heads):
            token_in(array, step).wait_recv()

    def joined(array, index):
        at, local = index // own_rows, index % own_rows
        return jnp.concatenate([tt[array, at, c, local] for c in range(cores)], axis=1)

    for index in range(rows):
        q_tok[index] = jnp.transpose(joined(0, index))
        da_tok[index] = jnp.transpose(joined(3, index))
        dk_acc[index] = jnp.zeros((width, keys), jnp.float32)
        dv_acc[index] = jnp.zeros((width, keys), jnp.float32)

    def queries(blk):
        mask = jnp.concatenate([mb[c] for c in range(cores)], axis=1).astype(jnp.float32)
        parts = [
            jnp.concatenate([bb[blk * pair + part, c] for c in range(cores)], axis=1)
            for part in range(pair)
        ]
        bias = jnp.concatenate(parts, axis=0).astype(jnp.float32)
        bias = bias + 1000000000.0 * (mask - 1.0)
        here = pl.ds(pl.multiple_of(blk * pair * block, 32), pair * block)
        total = None
        for index in range(rows):
            kt, vt = joined(1, index), joined(2, index)
            q, da = q_tok[index, here, :], da_tok[index, here, :]
            logits = nn(q, kt) * scaling + bias
            expo = jnp.exp(logits - jnp.max(logits, axis=-1, keepdims=True))
            probs = expo * (1.0 / jnp.sum(expo, axis=-1, keepdims=True))
            low = probs.astype(jnp.bfloat16)
            attended = nt(low, vt)
            inner = jnp.sum(da.astype(jnp.float32) * attended, axis=-1, keepdims=True)
            d_logits = probs * (nn(da, vt) - inner)
            d_low = d_logits.astype(jnp.bfloat16)
            dq_tok[index, here, :] = nt(d_low, kt) * scaling
            at_tok[index, here, :] = attended
            dk_acc[index] += tn(q, d_low)
            dv_acc[index] += tn(da, low)
            total = d_logits if total is None else total + d_logits
        for part in range(pair):
            rows_of = total[part * block : (part + 1) * block].astype(jnp.bfloat16)
            for c in range(cores):
                sb[blk * pair + part, c] = rows_of[:, c * tokens : (c + 1) * tokens]

    def partial_out(index, part):
        return remote(
            sb.at[index * pair + part], rb.at[zi, part], p_send.at[index, part],
            p_recv.at[zi, part], at_z(index),
        )

    orders = [
        sorted(range(groups), key=lambda b, a=a: abs(b - a) if b != a else groups)
        for a in range(groups)
    ]
    for distance in range(2, early + 1):
        relay(distance)

    def turn(step, carry):
        @pl.when(jnp.logical_and(step >= early, step < groups - 1))
        def _():
            relay(step + 1)

        index = jnp.int32(0)
        for a in range(groups):
            for s in range(groups):
                hit = jnp.logical_and(zi == a, step == s)
                index = jnp.where(hit, orders[a][s], index)
        queries(index)
        for part in range(pair):

            @pl.when(index != zi)
            def _(part=part):
                partial_out(index, part).start()

        return carry

    lax.fori_loop(0, groups, turn, 0)

    for index in range(rows):
        at, local = index // own_rows, index % own_rows
        whole = (
            jnp.transpose(dq_tok[index]),
            dk_acc[index] * scaling,
            dv_acc[index],
            jnp.transpose(at_tok[index]),
        )
        for array, value in enumerate(whole):
            value = value.astype(jnp.bfloat16)
            for c in range(cores):
                ot[at, c, array, local] = value[:, c * tokens : (c + 1) * tokens]

    def grads_out(step):
        to = lax.rem(me + step, heads)
        return remote(
            ot.at[to // cores, lax.rem(to, cores)], orecv.at[me],
            o_send.at[step], o_recv.at[step], at_quad(to),
        )

    def grads_in(step):
        src = lax.rem(me + heads - step, heads)
        return remote(
            ot.at[src // cores, lax.rem(src, cores)], orecv.at[src],
            o_send.at[step], o_recv.at[step], at_quad(src),
        )

    def sum_out(step):
        to = lax.rem(me + step, heads)
        return remote(
            gs.at[to // cores, lax.rem(to, cores)], gr.at[me],
            g_send.at[step], g_recv.at[step], at_quad(to),
        )

    def sum_in(step):
        src = lax.rem(me + heads - step, heads)
        return remote(
            gs.at[src // cores, lax.rem(src, cores)], gr.at[src],
            g_send.at[step], g_recv.at[step], at_quad(src),
        )

    for step in range(1, heads):
        grads_out(step).start()
    own_grads = pltpu.make_async_copy(ot.at[xi, core], orecv.at[me], local_sem.at[1])
    own_grads.start()

    for part in range(pair):
        for step in range(1, groups):
            src = lax.rem(zi + step, groups)
            remote(
                sb.at[zi * pair + part], rb.at[src, part], p_send.at[src, part],
                p_recv.at[src, part], at_z(src),
            ).wait_recv()
        for c in range(cores):
            value = sb[zi * pair + part, c].astype(jnp.float32)
            for step in range(1, groups):
                value += rb[lax.rem(zi + step, groups), part, c].astype(jnp.float32)
            gs[part, c] = value.astype(jnp.bfloat16)
    for step in range(1, heads):
        sum_out(step).start()
    own_sum = pltpu.make_async_copy(gs.at[xi, core], gr.at[me], local_sem.at[2])
    own_sum.start()

    for step in range(1, heads):
        grads_in(step).wait_recv()
        sum_in(step).wait_recv()
    own_grads.wait()
    own_sum.wait()
    for step in range(1, heads):
        bias_out_of(step).wait_send()
        grads_out(step).wait_send()
        sum_out(step).wait_send()
        for array in range(4):
            token_out(array, step).wait_send()
    for step in range(1, groups):
        for part in range(pair):
            partial_out(lax.rem(zi + step, groups), part).wait_send()
    for index in range(groups):
        for part in range(pair):

            @pl.when(jnp.logical_and(zi > 0, index >= zi))
            def _(at=index * pair + part):
                to_left(at).wait_send()

            @pl.when(jnp.logical_and(zi < groups - 1, index <= zi))
            def _(at=index * pair + part):
                to_right(at).wait_send()


def write_kernel(grads, sums, g_ref, o_ref, dq_ref, dk_ref, dv_ref, dg_ref, db_ref):
    heads = grads.shape[0]
    for local in range(g_ref.shape[0]):
        for array, ref in enumerate((dq_ref, dk_ref, dv_ref, dg_ref)):
            tall = jnp.concatenate([grads[head, array, local] for head in range(heads)], axis=0)
            value = jnp.transpose(tall)
            if array == 3:
                sig = jax.nn.sigmoid(g_ref[local].astype(jnp.float32))
                scale = o_ref[local].astype(jnp.float32) * sig * (1.0 - sig)
                value = (value.astype(jnp.float32) * scale).astype(jnp.bfloat16)
            ref[local] = value
    db_ref[...] = sums[...].astype(jnp.float32)


def fused(row_size, cores, query, keys, values, gate_logits, pair_bias, key_mask, grad_out):
    heads, block, tokens = pair_bias.shape
    own_rows, _, channels = query.shape
    pair = heads // cores
    groups = row_size // pair
    rows, width, whole = pair * own_rows, channels // heads, cores * tokens
    blocks = groups * pair
    low, full, dma = jnp.bfloat16, jnp.float32, pltpu.SemaphoreType.DMA
    grad = jax.ShapeDtypeStruct(query.shape, low)
    vmem, place = pl.BlockSpec(memory_space=pltpu.VMEM), pl.BlockSpec(memory_space=pl.ANY)
    grads, sums = pl.pallas_call(
        functools.partial(fused_kernel, groups, pair, cores),
        out_shape=(
            jax.ShapeDtypeStruct((heads, 4, own_rows, width, tokens), low),
            jax.ShapeDtypeStruct((heads, block, tokens), low),
        ),
        in_specs=[vmem] * 5 + [place, vmem],
        out_specs=[place] * 2,
        scratch_shapes=[
            pltpu.VMEM((4, heads, own_rows, width, tokens), low),
            pltpu.VMEM((4, pair, cores, own_rows, width, tokens), low),
            pltpu.VMEM((1, tokens), jnp.int32),
            pltpu.VMEM((cores, 1, tokens), jnp.int32),
            pltpu.VMEM((blocks, cores, block, tokens), low),
            pltpu.VMEM((rows, whole, width), low),
            pltpu.VMEM((rows, whole, width), low),
            pltpu.VMEM((rows, whole, width), full),
            pltpu.VMEM((rows, whole, width), full),
            pltpu.VMEM((rows, width, whole), full),
            pltpu.VMEM((rows, width, whole), full),
            pltpu.VMEM((blocks, cores, block, tokens), low),
            pltpu.VMEM((groups, pair, cores, block, tokens), low),
            pltpu.VMEM((pair, cores, block, tokens), low),
            pltpu.VMEM((pair, cores, 4, own_rows, width, tokens), low),
            dma((4, heads)), dma((4, heads)), dma((heads,)), dma((heads,)),
            dma((cores,)), dma((cores,)),
            dma((blocks,)), dma((blocks,)), dma((blocks,)),
            dma((groups, pair)), dma((groups, pair)),
            dma((heads,)), dma((heads,)), dma((heads,)), dma((heads,)), dma((3,)),
        ],
        compiler_params=pltpu.CompilerParams(
            collective_id=0, has_side_effects=True, vmem_limit_bytes=58 << 20
        ),
    )(query, keys, values, gate_logits, grad_out, pair_bias, key_mask)
    return pl.pallas_call(
        write_kernel,
        out_shape=(grad, grad, grad, grad, jax.ShapeDtypeStruct(pair_bias.shape, full)),
        in_specs=[vmem] * 4,
        out_specs=[vmem] * 5,
    )(grads, sums, gate_logits, grad_out)


def solution(mesh):
    in_specs = (
        P(("grp", "row"), "key", None),
        P(("grp", "row"), "key", None),
        P(("grp", "row"), "key", None),
        P(("grp", "row"), "key", None),
        P(None, ("grp", "row"), "key"),
        P(("grp", "key")),
        P(("grp", "row"), "key", None),
    )
    out_specs = (
        P(("grp", "row"), "key", None),
        P(("grp", "row"), "key", None),
        P(("grp", "row"), "key", None),
        P(("grp", "row"), "key", None),
        P(None, ("grp", "row"), "key"),
    )
    row_size, cores = mesh.shape["row"], mesh.shape["key"]

    def run(*arrays):
        heads, block, tokens = arrays[4].shape
        pair = max(heads // cores, 1)
        aligned = block % 32 == 0 and tokens % 128 == 0
        if aligned and heads == pair * cores and row_size % pair == 0:
            return fused(row_size, cores, *arrays)
        return shards(*arrays)

    return jax.shard_map(run, mesh=mesh, in_specs=in_specs, out_specs=out_specs, check_vma=False)
```

```python
import functools
import math

import jax
import jax.numpy as jnp
from jax import lax
from jax.experimental import pallas as pl
from jax.experimental.pallas import tpu as pltpu
from jax.sharding import PartitionSpec as P


def combined_all(value, axis, join):
    pieces = jax.tree.map(lambda part: lax.all_gather(part, axis), value)
    head = jax.tree.map(lambda part: part[0], pieces)
    tail = jax.tree.map(lambda part: part[1:], pieces)
    subtotal, _ = lax.scan(lambda subtotal, slab: (join(subtotal, slab), None), head, tail)
    return subtotal


def combine_stats(first, second):
    joint_max = jnp.maximum(first[0], second[0])
    joint_total = first[1] * jnp.exp(first[0] - joint_max) + second[1] * jnp.exp(
        second[0] - joint_max
    )
    return (joint_max, joint_total)


def shards(query, keys, values, gate_logits, pair_bias, key_mask, grad_out):
    row_count, key_count, channels = query.shape
    head_count = pair_bias.shape[0]
    head_size = channels // head_count
    scaling = 1.0 / math.sqrt(head_size)
    query_all, gate_all, cot_all = (
        lax.all_gather(query, "key", axis=1, tiled=True),
        lax.all_gather(gate_logits, "key", axis=1, tiled=True),
        lax.all_gather(grad_out, "key", axis=1, tiled=True),
    )
    query_count = query_all.shape[1]
    bias_all = lax.all_gather(pair_bias, "row", axis=1, tiled=True)
    mask_add = 1000000000.0 * (key_mask.astype(jnp.float32) - 1.0)
    bias_full = bias_all.astype(jnp.float32) + mask_add[None, None, :]

    def one_row(grad_acc, inputs):
        query_row, key_row, value_row, gate_row, cot_row, gate_own, cot_own = inputs
        query_heads = query_row.reshape(query_count, head_count, head_size)
        key_heads = key_row.reshape(key_count, head_count, head_size)
        value_heads = value_row.reshape(key_count, head_count, head_size)
        logits = (
            jnp.einsum("jhd,khd->hjk", query_heads, key_heads, preferred_element_type=jnp.float32)
            * scaling
            + bias_full
        )
        local_max = jnp.max(logits, axis=-1)
        local_total = jnp.sum(jnp.exp(logits - local_max[:, :, None]), axis=-1)
        row_max, row_total = combined_all((local_max, local_total), "key", combine_stats)
        softmax_out = jnp.exp(logits - row_max[:, :, None]) / row_total[:, :, None]
        softmax_low = softmax_out.astype(jnp.bfloat16)
        partial_out = jnp.einsum(
            "hjk,khd->jhd", softmax_low, value_heads, preferred_element_type=jnp.float32
        ).reshape(query_count, channels)
        gate_sig = jax.nn.sigmoid(gate_row.astype(jnp.float32))
        d_attended = (cot_row.astype(jnp.float32) * gate_sig).astype(jnp.bfloat16)
        upstream = d_attended.reshape(query_count, head_count, head_size)
        d_probs = jnp.einsum(
            "jhd,khd->hjk", upstream, value_heads, preferred_element_type=jnp.float32
        )
        own_out = lax.psum_scatter(partial_out, "key", scatter_dimension=0, tiled=True)
        inner = lax.psum(jnp.sum(softmax_low * d_probs, axis=-1), "key")
        own_sig = jax.nn.sigmoid(gate_own.astype(jnp.float32))
        gate_delta = (cot_own.astype(jnp.float32) * own_out * own_sig * (1.0 - own_sig)).astype(
            jnp.bfloat16
        )
        d_logits = softmax_out * (d_probs - inner[:, :, None])
        d_low = d_logits.astype(jnp.bfloat16)
        query_term = jnp.einsum(
            "hjk,khd->jhd", d_low, key_heads, preferred_element_type=jnp.float32
        ).reshape(query_count, channels)
        query_delta = (
            lax.psum_scatter(query_term, "key", scatter_dimension=0, tiled=True) * scaling
        ).astype(jnp.bfloat16)
        key_delta = (
            (
                jnp.einsum("hjk,jhd->khd", d_low, query_heads, preferred_element_type=jnp.float32)
                * scaling
            )
            .reshape(key_count, channels)
            .astype(jnp.bfloat16)
        )
        value_delta = (
            jnp.einsum("hjk,jhd->khd", softmax_low, upstream, preferred_element_type=jnp.float32)
            .reshape(key_count, channels)
            .astype(jnp.bfloat16)
        )
        return (grad_acc + d_logits, (query_delta, key_delta, value_delta, gate_delta))

    inputs_all = (query_all, keys, values, gate_all, cot_all, gate_logits, grad_out)
    empty_grad = jnp.zeros((head_count, query_count, key_count), jnp.float32)
    grad_acc, results = lax.scan(one_row, empty_grad, inputs_all)
    grad_bias = lax.psum_scatter(grad_acc, "row", scatter_dimension=1, tiled=True)
    return (results[0], results[1], results[2], results[3], grad_bias)


def nt(a, b):
    return lax.dot_general(a, b, (((1,), (1,)), ((), ())), preferred_element_type=jnp.float32)


def nn(a, b):
    return lax.dot_general(a, b, (((1,), (0,)), ((), ())), preferred_element_type=jnp.float32)


def tn(a, b):
    return lax.dot_general(a, b, (((0,), (0,)), ((), ())), preferred_element_type=jnp.float32)


def fused_kernel(
    groups, pair, cores,
    q_ref, k_ref, v_ref, g_ref, o_ref, bias_ref, mask_ref,
    orecv, gr,
    xt, tt, ms, mb, bb, q_tok, da_tok, dq_tok, at_tok, dk_acc, dv_acc, sb, rb, gs, ot,
    in_send, in_recv, bq_send, bq_recv, m_send, m_recv,
    bl_send, br_send, b_recv, p_send, p_recv, g_send, g_recv, o_send, o_recv, local_sem,
):
    row, core = lax.axis_index("row"), lax.axis_index("key")
    zi, xi = row // pair, lax.rem(row, pair)
    heads = pair * cores
    me = xi * cores + core
    own_rows, tokens, channels = q_ref.shape
    width = channels // heads
    rows = pair * own_rows
    keys = cores * tokens
    block = bias_ref.shape[1]
    scaling = 1.0 / math.sqrt(width)

    def at_quad(other):
        return {"row": zi * pair + other // cores, "key": lax.rem(other, cores)}

    def at_z(other):
        return {"row": other * pair + xi, "key": core}

    def remote(src, dst, send, recv, where):
        return pltpu.make_async_remote_copy(
            src_ref=src, dst_ref=dst, send_sem=send, recv_sem=recv,
            device_id=where, device_id_type=pl.DeviceIdType.MESH,
        )

    barrier = pltpu.get_barrier_semaphore()
    for step in range(1, heads):
        pl.semaphore_signal(
            barrier, inc=1, device_id=at_quad(lax.rem(me + step, heads)),
            device_id_type=pl.DeviceIdType.MESH,
        )
    for step in range(1, groups):
        pl.semaphore_signal(
            barrier, inc=1, device_id=at_z(lax.rem(zi + step, groups)),
            device_id_type=pl.DeviceIdType.MESH,
        )

    def turned(array):
        for local in range(own_rows):
            if array < 3:
                value = (q_ref, k_ref, v_ref)[array][local]
            else:
                sig = jax.nn.sigmoid(g_ref[local].astype(jnp.float32))
                value = (o_ref[local].astype(jnp.float32) * sig).astype(jnp.bfloat16)
            value = jnp.transpose(value)
            for head in range(heads):
                xt[array, head, local] = value[head * width : (head + 1) * width, :]

    own_bias = pltpu.make_async_copy(bias_ref.at[me], bb.at[row, core], local_sem.at[0])
    own_bias.start()
    ms[...] = mask_ref[...].reshape(1, tokens)
    turned(0)
    pl.semaphore_wait(barrier, heads - 1 + groups - 1)

    def bias_out_of(step):
        to = lax.rem(me + step, heads)
        return remote(
            bias_ref.at[to], bb.at[row, core], bq_send.at[step], bq_recv.at[me], at_quad(to)
        )

    def bias_from(src):
        return remote(
            bias_ref.at[src], bb.at[zi * pair + src // cores, lax.rem(src, cores)],
            bq_send.at[0], bq_recv.at[src], at_quad(src),
        )

    def mask_copy(other, src):
        return remote(
            ms, mb.at[src], m_send.at[other], m_recv.at[other],
            {"row": row, "key": lax.rem(core + other, cores)},
        )

    def token_out(array, step):
        to = lax.rem(me + step, heads)
        return remote(
            xt.at[array, to], tt.at[array, xi, core],
            in_send.at[array, step], in_recv.at[array, step], at_quad(to),
        )

    def token_in(array, step):
        src = lax.rem(me + heads - step, heads)
        return remote(
            xt.at[array, src], tt.at[array, src // cores, lax.rem(src, cores)],
            in_send.at[array, step], in_recv.at[array, step], at_quad(src),
        )

    def to_left(at):
        return remote(bb.at[at], bb.at[at], bl_send.at[at], b_recv.at[at], at_z(zi - 1))

    def to_right(at):
        return remote(bb.at[at], bb.at[at], br_send.at[at], b_recv.at[at], at_z(zi + 1))

    def launch(at):
        @pl.when(zi > 0)
        def _():
            to_left(at).start()

        @pl.when(zi < groups - 1)
        def _():
            to_right(at).start()

    def relay(distance):
        left, right = zi - distance, zi + distance
        for step in range(pair):
            part = lax.rem(xi + step, pair)

            @pl.when(left >= 0)
            def _(part=part):
                to_left(left * pair + part).wait_recv()

            @pl.when(jnp.logical_and(left >= 0, zi < groups - 1))
            def _(part=part):
                to_right(left * pair + part).start()

            @pl.when(right < groups)
            def _(part=part):
                to_right(right * pair + part).wait_recv()

            @pl.when(jnp.logical_and(right < groups, zi > 0))
            def _(part=part):
                to_left(right * pair + part).start()

    for step in range(1, heads):
        bias_out_of(step).start()
    for other in range(1, cores):
        mask_copy(other, core).start()
    mb[core] = ms[...]
    for step in range(1, heads):
        token_out(0, step).start()
    turned(1)
    for step in range(1, heads):
        token_out(1, step).start()
    own_bias.wait()
    for other in range(1, cores):
        bias_from(xi * cores + lax.rem(core + other, cores)).wait_recv()
    launch(row)
    for array in range(2, 4):
        turned(array)
        for step in range(1, heads):
            token_out(array, step).start()
    for step in range(1, pair):
        side = lax.rem(xi + step, pair)
        for other in range(cores):
            bias_from(side * cores + other).wait_recv()
        launch(zi * pair + side)
    for array in range(4):
        tt[array, xi, core] = xt[array, me]
    for other in range(1, cores):
        mask_copy(other, lax.rem(core + cores - other, cores)).wait()
    early = min(2, groups - 1)
    if early > 0:
        relay(1)
    for array in range(4):
        for step in range(1, heads):
            token_in(array, step).wait_recv()

    def joined(array, index):
        at, local = index // own_rows, index % own_rows
        return jnp.concatenate([tt[array, at, c, local] for c in range(cores)], axis=1)

    for index in range(rows):
        q_tok[index] = jnp.transpose(joined(0, index))
        da_tok[index] = jnp.transpose(joined(3, index))
        dk_acc[index] = jnp.zeros((width, keys), jnp.float32)
        dv_acc[index] = jnp.zeros((width, keys), jnp.float32)

    def queries(blk):
        mask = jnp.concatenate([mb[c] for c in range(cores)], axis=1).astype(jnp.float32)
        parts = [
            jnp.concatenate([bb[blk * pair + part, c] for c in range(cores)], axis=1)
            for part in range(pair)
        ]
        bias = jnp.concatenate(parts, axis=0).astype(jnp.float32)
        bias = bias + 1000000000.0 * (mask - 1.0)
        here = pl.ds(pl.multiple_of(blk * pair * block, 32), pair * block)
        total = None
        for index in range(rows):
            kt, vt = joined(1, index), joined(2, index)
            q, da = q_tok[index, here, :], da_tok[index, here, :]
            logits = nn(q, kt) * scaling + bias
            expo = jnp.exp(logits - jnp.max(logits, axis=-1, keepdims=True))
            probs = expo * (1.0 / jnp.sum(expo, axis=-1, keepdims=True))
            low = probs.astype(jnp.bfloat16)
            attended = nt(low, vt)
            inner = jnp.sum(da.astype(jnp.float32) * attended, axis=-1, keepdims=True)
            d_logits = probs * (nn(da, vt) - inner)
            d_low = d_logits.astype(jnp.bfloat16)
            dq_tok[index, here, :] = nt(d_low, kt) * scaling
            at_tok[index, here, :] = attended
            dk_acc[index] += tn(q, d_low)
            dv_acc[index] += tn(da, low)
            total = d_logits if total is None else total + d_logits
        for part in range(pair):
            rows_of = total[part * block : (part + 1) * block].astype(jnp.bfloat16)
            for c in range(cores):
                sb[blk * pair + part, c] = rows_of[:, c * tokens : (c + 1) * tokens]

    def partial_out(index, part):
        return remote(
            sb.at[index * pair + part], rb.at[zi, part], p_send.at[index, part],
            p_recv.at[zi, part], at_z(index),
        )

    orders = [
        sorted(range(groups), key=lambda b, a=a: abs(b - a) if b != a else groups)
        for a in range(groups)
    ]
    for distance in range(2, early + 1):
        relay(distance)

    def turn(step, carry):
        @pl.when(jnp.logical_and(step >= early, step < groups - 1))
        def _():
            relay(step + 1)

        index = jnp.int32(0)
        for a in range(groups):
            for s in range(groups):
                hit = jnp.logical_and(zi == a, step == s)
                index = jnp.where(hit, orders[a][s], index)
        queries(index)
        for part in range(pair):

            @pl.when(index != zi)
            def _(part=part):
                partial_out(index, lax.rem(xi + 1 + part, pair)).start()

        return carry

    lax.fori_loop(0, groups, turn, 0)

    for index in range(rows):
        at, local = index // own_rows, index % own_rows
        whole = (
            jnp.transpose(dq_tok[index]),
            dk_acc[index] * scaling,
            dv_acc[index],
            jnp.transpose(at_tok[index]),
        )
        for array, value in enumerate(whole):
            value = value.astype(jnp.bfloat16)
            for c in range(cores):
                ot[at, c, array, local] = value[:, c * tokens : (c + 1) * tokens]

    def grads_out(step):
        to = lax.rem(me + step, heads)
        return remote(
            ot.at[to // cores, lax.rem(to, cores)], orecv.at[me],
            o_send.at[step], o_recv.at[step], at_quad(to),
        )

    def grads_in(step):
        src = lax.rem(me + heads - step, heads)
        return remote(
            ot.at[src // cores, lax.rem(src, cores)], orecv.at[src],
            o_send.at[step], o_recv.at[step], at_quad(src),
        )

    def sum_out(step):
        to = lax.rem(me + step, heads)
        return remote(
            gs.at[to // cores, lax.rem(to, cores)], gr.at[me],
            g_send.at[step], g_recv.at[step], at_quad(to),
        )

    def sum_in(step):
        src = lax.rem(me + heads - step, heads)
        return remote(
            gs.at[src // cores, lax.rem(src, cores)], gr.at[src],
            g_send.at[step], g_recv.at[step], at_quad(src),
        )

    for step in range(1, heads):
        grads_out(step).start()
    own_grads = pltpu.make_async_copy(ot.at[xi, core], orecv.at[me], local_sem.at[1])
    own_grads.start()

    for turn_of in range(pair):
        part = lax.rem(xi + 1 + turn_of, pair)
        for step in range(1, groups):
            src = lax.rem(zi + step, groups)
            remote(
                sb.at[zi * pair + part], rb.at[src, part], p_send.at[src, part],
                p_recv.at[src, part], at_z(src),
            ).wait_recv()
        for c in range(cores):
            value = sb[zi * pair + part, c].astype(jnp.float32)
            for step in range(1, groups):
                value += rb[lax.rem(zi + step, groups), part, c].astype(jnp.float32)
            gs[part, c] = value.astype(jnp.bfloat16)
        if turn_of < pair - 1:
            for c in range(cores):
                sum_out(lax.rem(part * cores + c + heads - me, heads)).start()
        else:
            for c in range(1, cores):
                to = part * cores + lax.rem(core + c, cores)
                sum_out(lax.rem(to + heads - me, heads)).start()
    own_sum = pltpu.make_async_copy(gs.at[xi, core], gr.at[me], local_sem.at[2])
    own_sum.start()

    for step in range(1, heads):
        grads_in(step).wait_recv()
        sum_in(step).wait_recv()
    own_grads.wait()
    own_sum.wait()
    for step in range(1, heads):
        bias_out_of(step).wait_send()
        grads_out(step).wait_send()
        sum_out(step).wait_send()
        for array in range(4):
            token_out(array, step).wait_send()
    for step in range(1, groups):
        for part in range(pair):
            partial_out(lax.rem(zi + step, groups), part).wait_send()
    for index in range(groups):
        for part in range(pair):

            @pl.when(jnp.logical_and(zi > 0, index >= zi))
            def _(at=index * pair + part):
                to_left(at).wait_send()

            @pl.when(jnp.logical_and(zi < groups - 1, index <= zi))
            def _(at=index * pair + part):
                to_right(at).wait_send()


def write_kernel(grads, sums, g_ref, o_ref, dq_ref, dk_ref, dv_ref, dg_ref, db_ref):
    heads = grads.shape[0]
    for local in range(g_ref.shape[0]):
        for array, ref in enumerate((dq_ref, dk_ref, dv_ref, dg_ref)):
            tall = jnp.concatenate([grads[head, array, local] for head in range(heads)], axis=0)
            value = jnp.transpose(tall)
            if array == 3:
                sig = jax.nn.sigmoid(g_ref[local].astype(jnp.float32))
                scale = o_ref[local].astype(jnp.float32) * sig * (1.0 - sig)
                value = (value.astype(jnp.float32) * scale).astype(jnp.bfloat16)
            ref[local] = value
    db_ref[...] = sums[...].astype(jnp.float32)


def fused(row_size, cores, query, keys, values, gate_logits, pair_bias, key_mask, grad_out):
    heads, block, tokens = pair_bias.shape
    own_rows, _, channels = query.shape
    pair = heads // cores
    groups = row_size // pair
    rows, width, whole = pair * own_rows, channels // heads, cores * tokens
    blocks = groups * pair
    low, full, dma = jnp.bfloat16, jnp.float32, pltpu.SemaphoreType.DMA
    grad = jax.ShapeDtypeStruct(query.shape, low)
    vmem, place = pl.BlockSpec(memory_space=pltpu.VMEM), pl.BlockSpec(memory_space=pl.ANY)
    grads, sums = pl.pallas_call(
        functools.partial(fused_kernel, groups, pair, cores),
        out_shape=(
            jax.ShapeDtypeStruct((heads, 4, own_rows, width, tokens), low),
            jax.ShapeDtypeStruct((heads, block, tokens), low),
        ),
        in_specs=[vmem] * 5 + [place, vmem],
        out_specs=[place] * 2,
        scratch_shapes=[
            pltpu.VMEM((4, heads, own_rows, width, tokens), low),
            pltpu.VMEM((4, pair, cores, own_rows, width, tokens), low),
            pltpu.VMEM((1, tokens), jnp.int32),
            pltpu.VMEM((cores, 1, tokens), jnp.int32),
            pltpu.VMEM((blocks, cores, block, tokens), low),
            pltpu.VMEM((rows, whole, width), low),
            pltpu.VMEM((rows, whole, width), low),
            pltpu.VMEM((rows, whole, width), full),
            pltpu.VMEM((rows, whole, width), full),
            pltpu.VMEM((rows, width, whole), full),
            pltpu.VMEM((rows, width, whole), full),
            pltpu.VMEM((blocks, cores, block, tokens), low),
            pltpu.VMEM((groups, pair, cores, block, tokens), low),
            pltpu.VMEM((pair, cores, block, tokens), low),
            pltpu.VMEM((pair, cores, 4, own_rows, width, tokens), low),
            dma((4, heads)), dma((4, heads)), dma((heads,)), dma((heads,)),
            dma((cores,)), dma((cores,)),
            dma((blocks,)), dma((blocks,)), dma((blocks,)),
            dma((groups, pair)), dma((groups, pair)),
            dma((heads,)), dma((heads,)), dma((heads,)), dma((heads,)), dma((3,)),
        ],
        compiler_params=pltpu.CompilerParams(
            collective_id=0, has_side_effects=True, vmem_limit_bytes=58 << 20
        ),
    )(query, keys, values, gate_logits, grad_out, pair_bias, key_mask)
    return pl.pallas_call(
        write_kernel,
        out_shape=(grad, grad, grad, grad, jax.ShapeDtypeStruct(pair_bias.shape, full)),
        in_specs=[vmem] * 4,
        out_specs=[vmem] * 5,
    )(grads, sums, gate_logits, grad_out)


def solution(mesh):
    in_specs = (
        P(("grp", "row"), "key", None),
        P(("grp", "row"), "key", None),
        P(("grp", "row"), "key", None),
        P(("grp", "row"), "key", None),
        P(None, ("grp", "row"), "key"),
        P(("grp", "key")),
        P(("grp", "row"), "key", None),
    )
    out_specs = (
        P(("grp", "row"), "key", None),
        P(("grp", "row"), "key", None),
        P(("grp", "row"), "key", None),
        P(("grp", "row"), "key", None),
        P(None, ("grp", "row"), "key"),
    )
    row_size, cores = mesh.shape["row"], mesh.shape["key"]

    def run(*arrays):
        heads, block, tokens = arrays[4].shape
        pair = max(heads // cores, 1)
        aligned = block % 32 == 0 and tokens % 128 == 0
        if aligned and heads == pair * cores and row_size % pair == 0:
            return fused(row_size, cores, *arrays)
        return shards(*arrays)

    return jax.shard_map(run, mesh=mesh, in_specs=in_specs, out_specs=out_specs, check_vma=False)
```
